32 devices in a mesh: grp: 2 (over x), blk: 16 (over z, y, core).
Axes of the slice: x: 2, y: 2, z: 4, core: 2. Of those that a mesh axis runs over, the one named last changes fastest.
Arguments:
- queries: bfloat16 [32, 5120], P(('grp', 'blk')), parts along dimension 0, may hold values from -128 to 128
- home_device: int32 [8], P('grp'), parts along dimension 0, may hold values from 0 to 15, as said below
- lengths: int32 [8], P('grp'), parts along dimension 0, may hold values from 256 to 2048, as said below
- key_cache: bfloat16 [8, 2048, 1024], P('grp', 'blk'), parts along dimension 0, may hold values from -8 to 8
- value_cache: bfloat16 [8, 2048, 1024], P('grp', 'blk'), parts along dimension 0, may hold values from -6 to 6
- residual: bfloat16 [8, 5120], P('grp', 'blk'), parts along dimension 0, may hold values from -4 to 4
- out_weight: bfloat16 [5120, 5120], P('blk'), may hold values from -0.125 to 0.125
- ffn_gain: float32 [5120], replicated, may hold values from 0.5 to 1.5
- gate_weight: bfloat16 [5120, 27648], P(None, 'blk'), may hold values from -0.078125 to 0.078125
- up_weight: bfloat16 [5120, 27648], P(None, 'blk'), may hold values from -0.078125 to 0.078125
- down_weight: bfloat16 [27648, 5120], P('blk'), may hold values from -0.0546875 to 0.0546875
- query_gain: float32 [5120], replicated, may hold values from 0.5 to 1.5
- query_weight: bfloat16 [5120, 5120], P(None, 'blk'), may hold values from -0.078125 to 0.078125
- query_bias: float32 [5120], P('blk'), may hold values from -3 to 3
Outputs:
- hidden_out: bfloat16 [8, 5120], P('grp', 'blk'), parts along dimension 0
- next_queries: bfloat16 [32, 5120], P(('grp', 'blk')), parts along dimension 0
The draws below stay inside these ranges and needn't reach their ends.
There are 2 independent parts, one for each index of `grp`. The reference program is written for one: setup_inputs(seed, part) draws one part's arguments, and reference() takes and returns one part's arrays. A program takes and returns all parts, laid end to end along the dimension named above; an argument that names none is the same for every part. Nothing has to cross between parts.
Inputs may be any that keep to these rules, and one draw needn't show every extreme that they name: `home_device`: distinct device indices below 16; the last device is home to one sequence in every draw; rows of queries at devices that are home to no sequence are not read. `lengths`: one sequence of every draw has the full 2048 positions.
All inputs are finite; a program needn't handle non-finite values.
Results may differ from the reference program's by a relative error of at most 0.018.
Values may be sent and summed in bfloat16 or wider, within the bound.
A program may use at most 128 MiB of HBM per device.

```python
import jax
import jax.numpy as jnp
from jax import lax

D = 5120
HQ = 40
KVH = 8
HEAD = 128
FF = 27648
SEQS = 4
SHARDS = 16
CTX = 2048


def layout(key):
    folded = jax.random.fold_in(key, 4409)
    subkeys = jax.random.split(folded, 7)
    picked = jax.random.permutation(subkeys[0], SHARDS)[:SEQS].astype(jnp.int32)
    has_last = jnp.any(picked == SHARDS - 1)
    last_slot = jax.random.randint(subkeys[6], (), 0, SEQS)
    forced = jnp.where(jnp.arange(SEQS) == last_slot, SHARDS - 1, picked)
    homes_drawn = jnp.where(has_last, picked, forced).astype(jnp.int32)
    sampled = jax.random.randint(subkeys[1], (SEQS,), CTX // 8, CTX + 1)
    longest = jax.random.randint(subkeys[2], (), 0, SEQS)
    lengths = jnp.where(jnp.arange(SEQS) == longest, CTX, sampled).astype(jnp.int32)
    return (homes_drawn, lengths)


def draw_home_device(key, part):
    return layout(key)[0]


def draw_lengths(key, part):
    return layout(key)[1]


def draw_queries(key, part):
    jitter_key, scale_key = jax.random.split(jax.random.fold_in(key, 811), 2)
    jitter = jnp.clip(jax.random.normal(jitter_key, (SHARDS, HQ, HEAD), jnp.float32), -6.0, 6.0)
    head_scale = jnp.exp(jax.random.uniform(scale_key, (SHARDS, HQ, 1), jnp.float32, jnp.log(0.3), jnp.log(3.0)))
    drawn = (jitter * head_scale).reshape(SHARDS, HQ * HEAD)
    return drawn.astype(jnp.bfloat16)


def draw_key_cache(key, part):
    jitter = jnp.clip(jax.random.normal(jax.random.fold_in(key, 977), (SEQS, CTX, KVH, HEAD), jnp.float32), -6.0, 6.0)
    return jitter.reshape(SEQS, CTX, KVH * HEAD).astype(jnp.bfloat16)


def strengthened(drawn, key, source, target, parts, factor):
    def block_of(axis_at):
        return (jnp.arange(drawn.shape[axis_at]) // (drawn.shape[axis_at] // parts)).reshape((-1,) + (1,) * (drawn.ndim - 1 - axis_at))

    one_side = jax.random.permutation(key, parts)[block_of(target)]
    far = (block_of(target) + parts // 2) % parts
    return jnp.where((block_of(source) == one_side) | (block_of(source) == far), factor * drawn, drawn)


def steps_of(rng, extent, cuts, smallest, largest):
    factor_of = 1.0
    for dim, shards_of in cuts:
        heights = jax.random.uniform(jax.random.fold_in(jax.random.fold_in(rng, 6), dim), (shards_of,), jnp.float32, smallest / len(cuts), largest / len(cuts))
        factor_of = factor_of * jnp.repeat(jnp.exp(heights), extent[dim] // shards_of).reshape((-1,) + (1,) * (len(extent) - 1 - dim))
    return factor_of


def gaussian(own_key, extent, deviation, limit, pieces=(), kind=jnp.bfloat16):
    result = deviation * jax.random.normal(own_key, extent, jnp.float32)
    if pieces:
        result = result * steps_of(own_key, extent, pieces, -0.22, 0.18)
    return jnp.clip(result, -limit, limit).astype(kind)


def heavy_noise(rng, dims, scale, bound, cuts, heavy, kind=jnp.bfloat16):
    entries = scale * jax.random.normal(rng, dims, jnp.float32)
    if cuts:
        entries = entries * steps_of(rng, dims, cuts, -0.22, 0.18)
    return jnp.clip(strengthened(entries, jax.random.fold_in(rng, 3), *heavy), -bound, bound).astype(kind)


def setup_inputs(seed: int = 0, part: int = 0) -> dict:
    key_of = jax.random.split(jax.random.key(seed), 15)
    part_keys = jax.random.split(jax.random.fold_in(key_of[14], part), 15)
    return {
        "queries": draw_queries(jax.random.fold_in(jax.random.fold_in(key_of[14], part), 71), part),
        "home_device": draw_home_device(jax.random.fold_in(jax.random.fold_in(key_of[14], part), 71), part),
        "lengths": draw_lengths(jax.random.fold_in(jax.random.fold_in(key_of[14], part), 71), part),
        "key_cache": draw_key_cache(jax.random.fold_in(jax.random.fold_in(key_of[14], part), 71), part),
        "value_cache": gaussian(part_keys[4], (SEQS, CTX, KVH * HEAD), 1.0, 6.0, ((1, 16),)),
        "residual": gaussian(part_keys[5], (SEQS, D), 0.3, 4.0, ((1, 16),)),
        "out_weight": heavy_noise(key_of[6], (D, D), D ** -0.5, 0.125, ((0, 16),), (0, 1, 16, 2.0)),
        "ffn_gain": jnp.clip(1.0 + 0.1 * jax.random.normal(key_of[7], (D,), jnp.float32), 0.5, 1.5),
        "gate_weight": gaussian(key_of[8], (D, FF), D ** -0.5, 0.078125, ((1, 16),)),
        "up_weight": gaussian(key_of[9], (D, FF), D ** -0.5, 0.078125, ((1, 16),)),
        "down_weight": heavy_noise(key_of[10], (FF, D), FF ** -0.5, 0.0546875, ((0, 16),), (0, 1, 16, 2.0)),
        "query_gain": jnp.clip(1.0 + 0.1 * jax.random.normal(key_of[11], (D,), jnp.float32), 0.5, 1.5),
        "query_weight": gaussian(key_of[12], (D, D), D ** -0.5, 0.078125, ((1, 16),)),
        "query_bias": gaussian(key_of[13], (D,), 0.5, 3.0, ((0, 16),), jnp.float32),
    }


def attend(packed):
    query_row, key_rows, value_rows, length = packed
    group_size = HQ // KVH
    query_heads = query_row.astype(jnp.float32).reshape(KVH, group_size, HEAD)
    key_heads = key_rows.astype(jnp.float32).reshape(CTX, KVH, HEAD)
    value_heads = value_rows.astype(jnp.float32).reshape(CTX, KVH, HEAD)
    scores = jnp.einsum('kgd,tkd->kgt', query_heads, key_heads) * HEAD ** (-0.5)
    usable = (jnp.arange(CTX) < length)[None, None, :]
    masked = jnp.where(usable, scores, -1e+30)
    highest = lax.optimization_barrier(jnp.max(masked, axis=-1, keepdims=True))
    raised = jnp.where(usable, jnp.exp(masked - highest), 0.0)
    totals = lax.optimization_barrier(jnp.sum(raised, axis=-1))
    weights = lax.optimization_barrier(raised.astype(jnp.bfloat16)).astype(jnp.float32)
    summed = jnp.einsum('kgt,tkd->kgd', weights, value_heads)
    return (summed / totals[..., None]).reshape(D).astype(jnp.bfloat16)

def rms_scale(carried, gain_row):
    widened = carried.astype(jnp.float32)
    spread = lax.optimization_barrier(jnp.mean(widened * widened, axis=-1, keepdims=True))
    return (widened * lax.rsqrt(spread + 1e-06) * gain_row).astype(jnp.bfloat16)

def reference(queries, home_device, lengths, key_cache, value_cache, residual, out_weight, ffn_gain, gate_weight, up_weight, down_weight, query_gain, query_weight, query_bias):
    seq_rows = queries[home_device]
    context = lax.map(attend, (seq_rows, key_cache, value_cache, lengths))
    carried = (residual.astype(jnp.float32) + jnp.dot(context, out_weight, preferred_element_type=jnp.float32)).astype(jnp.bfloat16)
    ffn_input = rms_scale(carried, ffn_gain)
    gate_part = jnp.dot(ffn_input, gate_weight, preferred_element_type=jnp.float32)
    up_part = jnp.dot(ffn_input, up_weight, preferred_element_type=jnp.float32)
    activated = (jax.nn.silu(gate_part) * up_part).astype(jnp.bfloat16)
    hidden_out = (carried.astype(jnp.float32) + jnp.dot(activated, down_weight, preferred_element_type=jnp.float32)).astype(jnp.bfloat16)
    query_input = rms_scale(hidden_out, query_gain)
    fresh_query = (jnp.dot(query_input, query_weight, preferred_element_type=jnp.float32) + query_bias).astype(jnp.bfloat16)
    next_queries = jnp.zeros((SHARDS, D), jnp.bfloat16).at[home_device].set(fresh_query)
    return (hidden_out, next_queries)
```

```python
import functools

import jax
import jax.numpy as jnp
from jax import lax
from jax.experimental import pallas as pl
from jax.experimental.pallas import tpu as pltpu
from jax.sharding import PartitionSpec as P

HQ = 40
KVH = 8
HEAD = 128
GROUP = HQ // KVH
MESH = pl.DeviceIdType.MESH
F32 = jnp.float32
BF16 = jnp.bfloat16

ASK, MERGE, SUM_A, ROW_A, SUM_B, ROW_B, HOME = range(7)


def chunks_of(extent, unit, wanted):
    size = unit * max(1, wanted // unit)
    while extent % size:
        size -= unit
    return size


def kernel(
    n,
    home,
    length,
    queries,
    residual,
    ffn_gain,
    query_gain,
    query_bias,
    key_hbm,
    value_hbm,
    out_hbm,
    gate_hbm,
    up_hbm,
    down_hbm,
    query_hbm,
    hidden_out,
    next_out,
    keys,
    values,
    out_w,
    gate_w,
    up_w,
    down_w,
    query_w,
    asked,
    heads,
    flat,
    stats,
    merge_send,
    merge_recv,
    sum_send,
    sum_recv,
    row_send,
    row_recv,
    home_send,
    home_recv,
    wide,
    act_in,
    load_sem,
    gate_sem,
    up_sem,
    down_sem,
    send_sem,
    recv_sem,
):
    me = lax.axis_index("blk")
    seqs, feat = residual.shape
    width = queries.shape[1]
    span = keys.shape[1]
    packed = merge_send.shape[2]
    k_step = width // gate_sem.shape[0]
    n_step = width // down_sem.shape[0]

    loads = [
        pltpu.make_async_copy(src, dst, load_sem.at[i])
        for i, (src, dst) in enumerate(
            ((key_hbm, keys), (value_hbm, values), (out_hbm, out_w), (query_hbm, query_w))
        )
    ]

    def gate_load(c):
        rows = pl.ds(pl.multiple_of(c * k_step, k_step), k_step)
        return pltpu.make_async_copy(gate_hbm.at[rows, :], gate_w.at[rows, :], gate_sem.at[c])

    def up_load(c):
        rows = pl.ds(pl.multiple_of(c * k_step, k_step), k_step)
        return pltpu.make_async_copy(up_hbm.at[rows, :], up_w.at[rows, :], up_sem.at[c])

    def down_load(c):
        cols = pl.ds(pl.multiple_of(c * n_step, n_step), n_step)
        return pltpu.make_async_copy(down_hbm.at[:, cols], down_w.at[:, cols], down_sem.at[c])

    def each(low, high, action):
        def body(i, carry):
            action(i)
            return carry

        lax.fori_loop(low, high, body, 0)

    def start(phase, source, target):
        def send(off):
            peer = lax.rem(me + off, n)
            pltpu.make_async_remote_copy(
                src_ref=source(peer),
                dst_ref=target.at[me],
                send_sem=send_sem.at[phase],
                recv_sem=recv_sem.at[phase],
                device_id={"blk": peer},
                device_id_type=MESH,
            ).start()

        each(1, n, send)

    def finish(sem, phase, target):
        part = target.at[pl.ds(0, n - 1)]
        pltpu.make_async_copy(part, part, sem.at[phase]).wait()

    def arrive(phase, target):
        finish(recv_sem, phase, target)

    barrier = pltpu.get_barrier_semaphore()

    def greet(off):
        peer = lax.rem(me + off, n)
        pl.semaphore_signal(barrier, inc=1, device_id={"blk": peer}, device_id_type=MESH)

    each(1, n, greet)
    for load in loads[:3]:
        load.start()

    def both(c):
        gate_load(c).start()
        up_load(c).start()

    each(0, width // k_step, both)
    each(0, width // n_step, lambda c: down_load(c).start())
    loads[3].start()
    pl.semaphore_wait(barrier, n - 1)

    start(ASK, lambda peer: queries, asked)
    asked[me] = queries[...]
    heads[...] = jnp.zeros_like(heads)
    loads[0].wait()
    loads[1].wait()
    arrive(ASK, asked)

    pad = 8
    rows = KVH * pad
    position = me * span + lax.broadcasted_iota(jnp.int32, (rows, span), 1)
    at_row = lax.broadcasted_iota(jnp.int32, (rows, 128), 0)
    at_lane = lax.broadcasted_iota(jnp.int32, (rows, 128), 1)
    for s in range(seqs):
        line = asked[home[s]].astype(F32)
        for h in range(HQ):
            heads[s, h // GROUP, pl.ds(h % GROUP, 1), :] = line[:, h * HEAD : (h + 1) * HEAD]
        scores = jnp.concatenate(
            [
                lax.dot_general(
                    heads[s, k].astype(BF16),
                    keys[s, :, k * HEAD : (k + 1) * HEAD],
                    (((1,), (1,)), ((), ())),
                    preferred_element_type=F32,
                )
                for k in range(KVH)
            ],
            axis=0,
        ) * HEAD ** (-0.5)
        allowed = position < length[s]
        masked = jnp.where(allowed, scores, -1e30)
        peak = jnp.max(masked, axis=1, keepdims=True)
        raised = jnp.where(allowed, jnp.exp(masked - peak), 0.0)
        total = jnp.sum(raised, axis=1, keepdims=True)
        for k in range(KVH):
            mixed = jnp.dot(
                raised[k * pad : (k + 1) * pad].astype(BF16),
                values[s, :, k * HEAD : (k + 1) * HEAD],
                preferred_element_type=F32,
            )
            for g in range(GROUP):
                h = k * GROUP + g
                flat[pl.ds(s, 1), h * HEAD : (h + 1) * HEAD] = mixed[g : g + 1]
        spread = jnp.where(at_lane == at_row, peak, 0.0) + jnp.where(
            at_lane == at_row + rows, total, 0.0
        )
        stats[pl.ds(s, 1), :] = jnp.sum(spread, axis=0, keepdims=True)

    merge_send[...] = jnp.zeros_like(merge_send)
    for d in range(n):
        merge_send[d, :, 0:feat] = flat[:, d * feat : (d + 1) * feat]
        merge_send[d, :, packed - 128 : packed] = stats[...]
    start(MERGE, lambda peer: merge_send.at[peer], merge_recv)
    merge_recv[me] = merge_send[me]
    arrive(MERGE, merge_recv)

    stat = merge_recv[:, :, packed - 128 : packed]
    scale = jnp.exp(stat - jnp.max(stat, axis=0, keepdims=True))
    lane = lax.broadcasted_iota(jnp.int32, stat.shape, 2)
    first = (me * feat) // HEAD
    feature_head = (
        me * feat + lax.broadcasted_iota(jnp.int32, (n, seqs, feat), 2)
    ) // HEAD
    factor = jnp.zeros((n, seqs, feat), F32)
    for j in range((feat + HEAD - 2) // HEAD + 1):
        h = first + j
        slot = (h // GROUP) * pad + lax.rem(h, GROUP)
        own = jnp.sum(jnp.where(lane == slot, scale, 0.0), axis=2, keepdims=True)
        whole = jnp.sum(jnp.where(lane == slot + rows, stat, 0.0), axis=2, keepdims=True)
        share = own / jnp.sum(own * whole, axis=0, keepdims=True)
        factor = jnp.where(feature_head == h, share, factor)
    context = jnp.sum(merge_recv[:, :, 0:feat] * factor, axis=0).astype(BF16)

    def reduce_over(phase, buffers):
        for d in range(n):
            sum_send[buffers, d] = flat[:, d * feat : (d + 1) * feat]
        start(phase, lambda peer: sum_send.at[buffers, peer], sum_recv.at[buffers])
        sum_recv[buffers, me] = sum_send[buffers, me]
        arrive(phase, sum_recv.at[buffers])
        return jnp.sum(sum_recv[buffers], axis=0)

    def share_rows(phase, buffers, mine, gain):
        row_send[buffers] = mine
        start(phase, lambda peer: row_send.at[buffers], row_recv.at[buffers])
        row_recv[buffers, me] = mine
        arrive(phase, row_recv.at[buffers])
        for d in range(n):
            wide[:, d * feat : (d + 1) * feat] = row_recv[buffers, d].astype(F32)
        whole = wide[...]
        spread = jnp.mean(whole * whole, axis=-1, keepdims=True)
        act_in[...] = (whole * lax.rsqrt(spread + 1e-06) * gain[...]).astype(BF16)

    loads[2].wait()

    def project(c):
        cols = pl.ds(pl.multiple_of(c * n_step, n_step), n_step)
        flat[:, cols] = jnp.dot(context, out_w[:, cols], preferred_element_type=F32)

    each(0, width // n_step, project)
    carried = (residual[...].astype(F32) + reduce_over(SUM_A, 0)).astype(BF16)
    share_rows(ROW_A, 0, carried, ffn_gain)

    hidden = gate_w.shape[1]

    def expand(c, sums):
        gate_load(c).wait()
        up_load(c).wait()
        at = pl.ds(pl.multiple_of(c * k_step, k_step), k_step)
        piece = act_in[:, at]
        return (
            sums[0] + jnp.dot(piece, gate_w[at, :], preferred_element_type=F32),
            sums[1] + jnp.dot(piece, up_w[at, :], preferred_element_type=F32),
        )

    zero = jnp.zeros((seqs, hidden), F32)
    gate, up = lax.fori_loop(0, width // k_step, expand, (zero, zero))
    activated = (gate / (1.0 + jnp.exp(-gate)) * up).astype(BF16)

    def contract(c):
        down_load(c).wait()
        cols = pl.ds(pl.multiple_of(c * n_step, n_step), n_step)
        flat[:, cols] = jnp.dot(activated, down_w[:, cols], preferred_element_type=F32)

    each(0, width // n_step, contract)
    leaving = (carried.astype(F32) + reduce_over(SUM_B, 1)).astype(BF16)
    hidden_out[...] = leaving
    share_rows(ROW_B, 1, leaving, query_gain)

    loads[3].wait()

    def ask(c, total):
        at = pl.ds(pl.multiple_of(c * k_step, k_step), k_step)
        return total + jnp.dot(act_in[:, at], query_w[at, :], preferred_element_type=F32)

    fresh = lax.fori_loop(0, width // k_step, ask, jnp.zeros((seqs, feat), F32))
    fresh = (fresh + query_bias[...]).astype(BF16).astype(F32)

    def address(d):
        row = jnp.zeros((1, feat), F32)
        for s in range(seqs):
            row = row + jnp.where(home[s] == d, fresh[s : s + 1], 0.0)
        home_send[d] = row.astype(BF16)

    for d in range(n):
        address(d)
    start(HOME, lambda peer: home_send.at[peer], home_recv)
    home_recv[me] = home_send[me]
    arrive(HOME, home_recv)
    for d in range(n):
        wide[0:1, d * feat : (d + 1) * feat] = home_recv[d].astype(F32)
    next_out[...] = wide[0:1, :].astype(BF16)

    finish(send_sem, ASK, asked)
    finish(send_sem, MERGE, merge_recv)
    finish(send_sem, SUM_A, sum_recv.at[0])
    finish(send_sem, ROW_A, row_recv.at[0])
    finish(send_sem, SUM_B, sum_recv.at[1])
    finish(send_sem, ROW_B, row_recv.at[1])
    finish(send_sem, HOME, home_recv)


def local(
    n,
    queries,
    home_device,
    lengths,
    key_cache,
    value_cache,
    residual,
    out_weight,
    ffn_gain,
    gate_weight,
    up_weight,
    down_weight,
    query_gain,
    query_weight,
    query_bias,
):
    seqs, feat = residual.shape
    width = queries.shape[1]
    packed = pl.cdiv(feat, 128) * 128 + 128
    step = chunks_of(width, 128, 512)
    vmem = pl.BlockSpec(memory_space=pltpu.VMEM)
    smem = pl.BlockSpec(memory_space=pltpu.SMEM)
    left = pl.BlockSpec(memory_space=pl.ANY)
    dma = pltpu.SemaphoreType.DMA

    def like(array):
        return pltpu.VMEM(array.shape, array.dtype)

    return pl.pallas_call(
        functools.partial(kernel, n),
        out_shape=(
            jax.ShapeDtypeStruct((seqs, feat), BF16),
            jax.ShapeDtypeStruct((1, width), BF16),
        ),
        in_specs=[smem] * 2 + [vmem] * 5 + [left] * 7,
        out_specs=(vmem, vmem),
        scratch_shapes=[
            like(key_cache),
            like(value_cache),
            like(out_weight),
            like(gate_weight),
            like(up_weight),
            like(down_weight),
            like(query_weight),
            pltpu.VMEM((n, 1, width), BF16),
            pltpu.VMEM((seqs, KVH, 8, HEAD), F32),
            pltpu.VMEM((seqs, width), F32),
            pltpu.VMEM((seqs, 128), F32),
            pltpu.VMEM((n, seqs, packed), F32),
            pltpu.VMEM((n, seqs, packed), F32),
            pltpu.VMEM((2, n, seqs, feat), F32),
            pltpu.VMEM((2, n, seqs, feat), F32),
            pltpu.VMEM((2, seqs, feat), BF16),
            pltpu.VMEM((2, n, seqs, feat), BF16),
            pltpu.VMEM((n, 1, feat), BF16),
            pltpu.VMEM((n, 1, feat), BF16),
            pltpu.VMEM((seqs, width), F32),
            pltpu.VMEM((seqs, width), BF16),
            dma((4,)),
            dma((width // step,)),
            dma((width // step,)),
            dma((width // step,)),
            dma((7,)),
            dma((7,)),
        ],
        compiler_params=pltpu.CompilerParams(
            collective_id=0, has_side_effects=True, vmem_limit_bytes=67043328
        ),
        name="decode_step",
    )(
        home_device,
        lengths,
        queries,
        residual,
        ffn_gain[None, :],
        query_gain[None, :],
        query_bias[None, :],
        key_cache,
        value_cache,
        out_weight,
        gate_weight,
        up_weight,
        down_weight,
        query_weight,
    )


def solution(mesh):
    placed = (
        P(("grp", "blk"), None),
        P("grp"),
        P("grp"),
        P("grp", "blk", None),
        P("grp", "blk", None),
        P("grp", "blk"),
        P("blk", None),
        P(),
        P(None, "blk"),
        P(None, "blk"),
        P("blk", None),
        P(),
        P(None, "blk"),
        P("blk"),
    )
    return jax.shard_map(
        functools.partial(local, mesh.shape["blk"]),
        mesh=mesh,
        in_specs=placed,
        out_specs=(P("grp", "blk"), P(("grp", "blk"), None)),
        check_vma=False,
    )
```

```python
import functools

import jax
import jax.numpy as jnp
from jax import lax
from jax.experimental import pallas as pl
from jax.experimental.pallas import tpu as pltpu
from jax.sharding import PartitionSpec as P

HQ = 40
KVH = 8
HEAD = 128
GROUP = HQ // KVH
MESH = pl.DeviceIdType.MESH
F32 = jnp.float32
BF16 = jnp.bfloat16

ASK, MERGE, SUM_A, ROW_A, SUM_B, ROW_B, HOME = range(7)


def chunks_of(extent, unit, wanted):
    size = unit * max(1, wanted // unit)
    while extent % size:
        size -= unit
    return size


def dot_rows(left, right):
    return lax.dot_general(
        left, right, (((1,), (1,)), ((), ())), preferred_element_type=F32
    )


def kernel(
    n,
    home,
    length,
    queries,
    residual,
    ffn_gain,
    query_gain,
    query_bias,
    key_hbm,
    value_hbm,
    out_hbm,
    gate_hbm,
    up_hbm,
    down_hbm,
    query_hbm,
    hidden_out,
    next_out,
    keys,
    values,
    out_w,
    gate_w,
    up_w,
    down_w,
    query_w,
    asked,
    heads,
    flat,
    stats,
    merge_send,
    merge_recv,
    sum_send,
    sum_recv,
    row_send,
    row_recv,
    home_send,
    home_recv,
    wide,
    act_in,
    load_sem,
    gate_sem,
    up_sem,
    down_sem,
    send_sem,
    recv_sem,
):
    me = lax.axis_index("blk")
    seqs, feat = residual.shape
    width = queries.shape[1]
    span = keys.shape[1]
    packed = merge_send.shape[2]
    k_step = width // gate_sem.shape[0]
    n_step = width // down_sem.shape[0]

    loads = [
        pltpu.make_async_copy(src, dst, load_sem.at[i])
        for i, (src, dst) in enumerate(
            ((key_hbm, keys), (value_hbm, values), (out_hbm, out_w), (query_hbm, query_w))
        )
    ]

    def gate_load(c):
        cols = pl.ds(pl.multiple_of(c * k_step, k_step), k_step)
        return pltpu.make_async_copy(gate_hbm.at[:, cols], gate_w.at[:, cols], gate_sem.at[c])

    def up_load(c):
        cols = pl.ds(pl.multiple_of(c * k_step, k_step), k_step)
        return pltpu.make_async_copy(up_hbm.at[:, cols], up_w.at[:, cols], up_sem.at[c])

    def down_load(c):
        cols = pl.ds(pl.multiple_of(c * n_step, n_step), n_step)
        return pltpu.make_async_copy(down_hbm.at[:, cols], down_w.at[:, cols], down_sem.at[c])

    def each(low, high, action):
        def body(i, carry):
            action(i)
            return carry

        lax.fori_loop(low, high, body, 0)

    def start(phase, source, target):
        def send(off):
            peer = lax.rem(me + off, n)
            pltpu.make_async_remote_copy(
                src_ref=source(peer),
                dst_ref=target.at[me],
                send_sem=send_sem.at[phase],
                recv_sem=recv_sem.at[phase],
                device_id={"blk": peer},
                device_id_type=MESH,
            ).start()

        each(1, n, send)

    def finish(sem, phase, target):
        part = target.at[pl.ds(0, n - 1)]
        pltpu.make_async_copy(part, part, sem.at[phase]).wait()

    def arrive(phase, target):
        finish(recv_sem, phase, target)

    barrier = pltpu.get_barrier_semaphore()

    def greet(off):
        peer = lax.rem(me + off, n)
        pl.semaphore_signal(barrier, inc=1, device_id={"blk": peer}, device_id_type=MESH)

    each(1, n, greet)
    for load in loads[:3]:
        load.start()

    def both(c):
        gate_load(c).start()
        up_load(c).start()

    each(0, width // k_step, both)
    each(0, width // n_step, lambda c: down_load(c).start())
    loads[3].start()
    pl.semaphore_wait(barrier, n - 1)

    start(ASK, lambda peer: queries, asked)
    asked[me] = queries[...]
    heads[...] = jnp.zeros_like(heads)
    loads[0].wait()
    loads[1].wait()
    arrive(ASK, asked)

    pad = 8
    rows = KVH * pad
    position = me * span + lax.broadcasted_iota(jnp.int32, (rows, span), 1)
    at_row = lax.broadcasted_iota(jnp.int32, (rows, 128), 0)
    at_lane = lax.broadcasted_iota(jnp.int32, (rows, 128), 1)
    for s in range(seqs):
        line = asked[home[s]].astype(F32)
        for h in range(HQ):
            heads[s, h // GROUP, pl.ds(h % GROUP, 1), :] = line[:, h * HEAD : (h + 1) * HEAD]
        scores = jnp.concatenate(
            [
                dot_rows(heads[s, k].astype(BF16), keys[s, :, k * HEAD : (k + 1) * HEAD])
                for k in range(KVH)
            ],
            axis=0,
        ) * HEAD ** (-0.5)
        allowed = position < length[s]
        masked = jnp.where(allowed, scores, -1e30)
        peak = jnp.max(masked, axis=1, keepdims=True)
        raised = jnp.where(allowed, jnp.exp(masked - peak), 0.0)
        total = jnp.sum(raised, axis=1, keepdims=True)
        for k in range(KVH):
            mixed = jnp.dot(
                raised[k * pad : (k + 1) * pad].astype(BF16),
                values[s, :, k * HEAD : (k + 1) * HEAD],
                preferred_element_type=F32,
            )
            for g in range(GROUP):
                h = k * GROUP + g
                flat[pl.ds(s, 1), h * HEAD : (h + 1) * HEAD] = mixed[g : g + 1]
        spread = jnp.where(at_lane == at_row, peak, 0.0) + jnp.where(
            at_lane == at_row + rows, total, 0.0
        )
        stats[pl.ds(s, 1), :] = jnp.sum(spread, axis=0, keepdims=True)

    merge_send[...] = jnp.zeros_like(merge_send)
    for d in range(n):
        merge_send[d, :, 0:feat] = flat[:, d * feat : (d + 1) * feat]
        merge_send[d, :, packed - 128 : packed] = stats[...]
    start(MERGE, lambda peer: merge_send.at[peer], merge_recv)
    merge_recv[me] = merge_send[me]
    arrive(MERGE, merge_recv)

    stat = merge_recv[:, :, packed - 128 : packed]
    scale = jnp.exp(stat - jnp.max(stat, axis=0, keepdims=True))
    lane = lax.broadcasted_iota(jnp.int32, stat.shape, 2)
    first = (me * feat) // HEAD
    feature_head = (
        me * feat + lax.broadcasted_iota(jnp.int32, (n, seqs, feat), 2)
    ) // HEAD
    factor = jnp.zeros((n, seqs, feat), F32)
    for j in range((feat + HEAD - 2) // HEAD + 1):
        h = first + j
        slot = (h // GROUP) * pad + lax.rem(h, GROUP)
        own = jnp.sum(jnp.where(lane == slot, scale, 0.0), axis=2, keepdims=True)
        whole = jnp.sum(jnp.where(lane == slot + rows, stat, 0.0), axis=2, keepdims=True)
        share = own / jnp.sum(own * whole, axis=0, keepdims=True)
        factor = jnp.where(feature_head == h, share, factor)
    context = jnp.sum(merge_recv[:, :, 0:feat] * factor, axis=0).astype(BF16)

    def reduce_over(phase, buffers):
        for d in range(n):
            sum_send[buffers, d] = flat[:, d * feat : (d + 1) * feat]
        start(phase, lambda peer: sum_send.at[buffers, peer], sum_recv.at[buffers])
        sum_recv[buffers, me] = sum_send[buffers, me]
        arrive(phase, sum_recv.at[buffers])
        return jnp.sum(sum_recv[buffers], axis=0)

    def share_rows(phase, buffers, mine, gain):
        row_send[buffers] = mine
        start(phase, lambda peer: row_send.at[buffers], row_recv.at[buffers])
        row_recv[buffers, me] = mine
        arrive(phase, row_recv.at[buffers])
        for d in range(n):
            wide[:, d * feat : (d + 1) * feat] = row_recv[buffers, d].astype(F32)
        whole = wide[...]
        spread = jnp.mean(whole * whole, axis=-1, keepdims=True)
        act_in[...] = (whole * lax.rsqrt(spread + 1e-06) * gain[...]).astype(BF16)

    loads[2].wait()

    def project(c):
        cols = pl.ds(pl.multiple_of(c * n_step, n_step), n_step)
        flat[:, cols] = jnp.dot(context, out_w[:, cols], preferred_element_type=F32)

    each(0, width // n_step, project)
    carried = (residual[...].astype(F32) + reduce_over(SUM_A, 0)).astype(BF16)
    share_rows(ROW_A, 0, carried, ffn_gain)

    hidden = gate_w.shape[0]

    def expand(c, sums):
        gate_load(c).wait()
        up_load(c).wait()
        at = pl.ds(pl.multiple_of(c * k_step, k_step), k_step)
        piece = act_in[:, at]
        return (
            sums[0] + dot_rows(piece, gate_w[:, at]),
            sums[1] + dot_rows(piece, up_w[:, at]),
        )

    zero = jnp.zeros((seqs, hidden), F32)
    gate, up = lax.fori_loop(0, width // k_step, expand, (zero, zero))
    activated = (gate / (1.0 + jnp.exp(-gate)) * up).astype(BF16)

    def contract(c):
        down_load(c).wait()
        cols = pl.ds(pl.multiple_of(c * n_step, n_step), n_step)
        flat[:, cols] = jnp.dot(activated, down_w[:, cols], preferred_element_type=F32)

    each(0, width // n_step, contract)
    leaving = (carried.astype(F32) + reduce_over(SUM_B, 1)).astype(BF16)
    hidden_out[...] = leaving
    share_rows(ROW_B, 1, leaving, query_gain)

    loads[3].wait()

    def ask(c, total):
        at = pl.ds(pl.multiple_of(c * k_step, k_step), k_step)
        return total + dot_rows(act_in[:, at], query_w[:, at])

    fresh = lax.fori_loop(0, width // k_step, ask, jnp.zeros((seqs, feat), F32))
    fresh = (fresh + query_bias[...]).astype(BF16).astype(F32)

    def address(d):
        row = jnp.zeros((1, feat), F32)
        for s in range(seqs):
            row = row + jnp.where(home[s] == d, fresh[s : s + 1], 0.0)
        home_send[d] = row.astype(BF16)

    for d in range(n):
        address(d)
    start(HOME, lambda peer: home_send.at[peer], home_recv)
    home_recv[me] = home_send[me]
    arrive(HOME, home_recv)
    for d in range(n):
        wide[0:1, d * feat : (d + 1) * feat] = home_recv[d].astype(F32)
    next_out[...] = wide[0:1, :].astype(BF16)

    finish(send_sem, ASK, asked)
    finish(send_sem, MERGE, merge_recv)
    finish(send_sem, SUM_A, sum_recv.at[0])
    finish(send_sem, ROW_A, row_recv.at[0])
    finish(send_sem, SUM_B, sum_recv.at[1])
    finish(send_sem, ROW_B, row_recv.at[1])
    finish(send_sem, HOME, home_recv)


def local(
    n,
    queries,
    home_device,
    lengths,
    key_cache,
    value_cache,
    residual,
    out_weight,
    ffn_gain,
    gate_weight,
    up_weight,
    down_weight,
    query_gain,
    query_weight,
    query_bias,
):
    seqs, feat = residual.shape
    width = queries.shape[1]
    packed = pl.cdiv(feat, 128) * 128 + 128
    step = chunks_of(width, 128, 512)
    vmem = pl.BlockSpec(memory_space=pltpu.VMEM)
    smem = pl.BlockSpec(memory_space=pltpu.SMEM)
    left = pl.BlockSpec(memory_space=pl.ANY)
    dma = pltpu.SemaphoreType.DMA

    def like(array):
        return pltpu.VMEM(array.shape, array.dtype)

    def flipped(array):
        return pltpu.VMEM(array.shape[::-1], array.dtype)

    return pl.pallas_call(
        functools.partial(kernel, n),
        out_shape=(
            jax.ShapeDtypeStruct((seqs, feat), BF16),
            jax.ShapeDtypeStruct((1, width), BF16),
        ),
        in_specs=[smem] * 2 + [vmem] * 5 + [left] * 7,
        out_specs=(vmem, vmem),
        scratch_shapes=[
            like(key_cache),
            like(value_cache),
            like(out_weight),
            flipped(gate_weight),
            flipped(up_weight),
            like(down_weight),
            flipped(query_weight),
            pltpu.VMEM((n, 1, width), BF16),
            pltpu.VMEM((seqs, KVH, 8, HEAD), F32),
            pltpu.VMEM((seqs, width), F32),
            pltpu.VMEM((seqs, 128), F32),
            pltpu.VMEM((n, seqs, packed), F32),
            pltpu.VMEM((n, seqs, packed), F32),
            pltpu.VMEM((2, n, seqs, feat), F32),
            pltpu.VMEM((2, n, seqs, feat), F32),
            pltpu.VMEM((2, seqs, feat), BF16),
            pltpu.VMEM((2, n, seqs, feat), BF16),
            pltpu.VMEM((n, 1, feat), BF16),
            pltpu.VMEM((n, 1, feat), BF16),
            pltpu.VMEM((seqs, width), F32),
            pltpu.VMEM((seqs, width), BF16),
            dma((4,)),
            dma((width // step,)),
            dma((width // step,)),
            dma((width // step,)),
            dma((7,)),
            dma((7,)),
        ],
        compiler_params=pltpu.CompilerParams(
            collective_id=0, has_side_effects=True, vmem_limit_bytes=67043328
        ),
        name="decode_step",
    )(
        home_device,
        lengths,
        queries,
        residual,
        ffn_gain[None, :],
        query_gain[None, :],
        query_bias[None, :],
        key_cache,
        value_cache,
        out_weight,
        gate_weight.T,
        up_weight.T,
        down_weight,
        query_weight.T,
    )


def solution(mesh):
    placed = (
        P(("grp", "blk"), None),
        P("grp"),
        P("grp"),
        P("grp", "blk", None),
        P("grp", "blk", None),
        P("grp", "blk"),
        P("blk", None),
        P(),
        P(None, "blk"),
        P(None, "blk"),
        P("blk", None),
        P(),
        P(None, "blk"),
        P("blk"),
    )
    return jax.shard_map(
        functools.partial(local, mesh.shape["blk"]),
        mesh=mesh,
        in_specs=placed,
        out_specs=(P("grp", "blk"), P(("grp", "blk"), None)),
        check_vma=False,
    )
```

```python
import functools

import jax
import jax.numpy as jnp
from jax import lax
from jax.experimental import pallas as pl
from jax.experimental.pallas import tpu as pltpu
from jax.sharding import PartitionSpec as P

HQ = 40
KVH = 8
HEAD = 128
GROUP = HQ // KVH
MESH = pl.DeviceIdType.MESH
F32 = jnp.float32
BF16 = jnp.bfloat16

ASK, MERGE, SUM_A, ROW_A, SUM_B, ROW_B, HOME = range(7)


def chunks_of(extent, unit, wanted):
    size = unit * max(1, wanted // unit)
    while extent % size:
        size -= unit
    return size


def dot_rows(left, right):
    return lax.dot_general(
        left, right, (((1,), (1,)), ((), ())), preferred_element_type=F32
    )


def kernel(
    n,
    home,
    length,
    queries,
    residual,
    ffn_gain,
    query_gain,
    query_bias,
    key_hbm,
    value_hbm,
    out_hbm,
    gate_hbm,
    up_hbm,
    down_hbm,
    query_hbm,
    hidden_out,
    next_out,
    keys,
    values,
    out_w,
    gate_w,
    up_w,
    down_w,
    query_w,
    asked,
    heads,
    flat,
    stats,
    merge_send,
    merge_recv,
    sum_send,
    sum_recv,
    row_send,
    row_recv,
    home_send,
    home_recv,
    wide,
    act_in,
    load_sem,
    gate_sem,
    up_sem,
    down_sem,
    send_sem,
    recv_sem,
):
    me = lax.axis_index("blk")
    seqs, feat = residual.shape
    width = queries.shape[1]
    span = keys.shape[1]
    packed = merge_send.shape[2]
    k_step = width // gate_sem.shape[0]
    n_step = width // down_sem.shape[0]

    loads = [
        pltpu.make_async_copy(src, dst, load_sem.at[i])
        for i, (src, dst) in enumerate(
            ((key_hbm, keys), (value_hbm, values), (out_hbm, out_w), (query_hbm, query_w))
        )
    ]

    def gate_load(c):
        cols = pl.ds(pl.multiple_of(c * k_step, k_step), k_step)
        return pltpu.make_async_copy(gate_hbm.at[:, cols], gate_w.at[:, cols], gate_sem.at[c])

    def up_load(c):
        cols = pl.ds(pl.multiple_of(c * k_step, k_step), k_step)
        return pltpu.make_async_copy(up_hbm.at[:, cols], up_w.at[:, cols], up_sem.at[c])

    def down_load(c):
        cols = pl.ds(pl.multiple_of(c * n_step, n_step), n_step)
        return pltpu.make_async_copy(down_hbm.at[:, cols], down_w.at[:, cols], down_sem.at[c])

    def each(low, high, action):
        def body(i, carry):
            action(i)
            return carry

        lax.fori_loop(low, high, body, 0, unroll=high - low <= 16)

    def start(phase, source, target):
        def send(off):
            peer = lax.rem(me + off, n)
            pltpu.make_async_remote_copy(
                src_ref=source(peer),
                dst_ref=target.at[me],
                send_sem=send_sem.at[phase],
                recv_sem=recv_sem.at[phase],
                device_id={"blk": peer},
                device_id_type=MESH,
            ).start()

        each(1, n, send)

    def finish(sem, phase, target):
        part = target.at[pl.ds(0, n - 1)]
        pltpu.make_async_copy(part, part, sem.at[phase]).wait()

    def arrive(phase, target):
        finish(recv_sem, phase, target)

    barrier = pltpu.get_barrier_semaphore()

    def greet(off):
        peer = lax.rem(me + off, n)
        pl.semaphore_signal(barrier, inc=1, device_id={"blk": peer}, device_id_type=MESH)

    each(1, n, greet)
    for load in loads[:3]:
        load.start()

    def both(c):
        gate_load(c).start()
        up_load(c).start()

    pl.semaphore_wait(barrier, n - 1)

    start(ASK, lambda peer: queries, asked)
    each(0, width // k_step, both)
    each(0, width // n_step, lambda c: down_load(c).start())
    loads[3].start()
    asked[me] = queries[...]
    heads[...] = jnp.zeros_like(heads)
    loads[0].wait()
    loads[1].wait()
    arrive(ASK, asked)

    pad = 8
    rows = KVH * pad
    position = me * span + lax.broadcasted_iota(jnp.int32, (rows, span), 1)
    at_row = lax.broadcasted_iota(jnp.int32, (rows, 128), 0)
    at_lane = lax.broadcasted_iota(jnp.int32, (rows, 128), 1)
    for s in range(seqs):
        line = asked[home[s]].astype(F32)
        for h in range(HQ):
            heads[s, h // GROUP, pl.ds(h % GROUP, 1), :] = line[:, h * HEAD : (h + 1) * HEAD]
        scores = jnp.concatenate(
            [
                dot_rows(heads[s, k].astype(BF16), keys[s, :, k * HEAD : (k + 1) * HEAD])
                for k in range(KVH)
            ],
            axis=0,
        ) * HEAD ** (-0.5)
        allowed = position < length[s]
        masked = jnp.where(allowed, scores, -1e30)
        peak = jnp.max(masked, axis=1, keepdims=True)
        raised = jnp.where(allowed, jnp.exp(masked - peak), 0.0)
        total = jnp.sum(raised, axis=1, keepdims=True)
        for k in range(KVH):
            mixed = jnp.dot(
                raised[k * pad : (k + 1) * pad].astype(BF16),
                values[s, :, k * HEAD : (k + 1) * HEAD],
                preferred_element_type=F32,
            )
            for g in range(GROUP):
                h = k * GROUP + g
                flat[pl.ds(s, 1), h * HEAD : (h + 1) * HEAD] = mixed[g : g + 1]
        spread = jnp.where(at_lane == at_row, peak, 0.0) + jnp.where(
            at_lane == at_row + rows, total, 0.0
        )
        stats[pl.ds(s, 1), :] = jnp.sum(spread, axis=0, keepdims=True)

    merge_send[...] = jnp.zeros_like(merge_send)
    for d in range(n):
        merge_send[d, :, 0:feat] = flat[:, d * feat : (d + 1) * feat]
        merge_send[d, :, packed - 128 : packed] = stats[...]
    start(MERGE, lambda peer: merge_send.at[peer], merge_recv)
    merge_recv[me] = merge_send[me]
    arrive(MERGE, merge_recv)

    stat = merge_recv[:, :, packed - 128 : packed]
    scale = jnp.exp(stat - jnp.max(stat, axis=0, keepdims=True))
    lane = lax.broadcasted_iota(jnp.int32, stat.shape, 2)
    first = (me * feat) // HEAD
    feature_head = (
        me * feat + lax.broadcasted_iota(jnp.int32, (n, seqs, feat), 2)
    ) // HEAD
    factor = jnp.zeros((n, seqs, feat), F32)
    for j in range((feat + HEAD - 2) // HEAD + 1):
        h = first + j
        slot = (h // GROUP) * pad + lax.rem(h, GROUP)
        own = jnp.sum(jnp.where(lane == slot, scale, 0.0), axis=2, keepdims=True)
        whole = jnp.sum(jnp.where(lane == slot + rows, stat, 0.0), axis=2, keepdims=True)
        share = own / jnp.sum(own * whole, axis=0, keepdims=True)
        factor = jnp.where(feature_head == h, share, factor)
    context = jnp.sum(merge_recv[:, :, 0:feat] * factor, axis=0).astype(BF16)

    def reduce_over(phase, buffers):
        for d in range(n):
            sum_send[buffers, d] = flat[:, d * feat : (d + 1) * feat].astype(BF16)
        start(phase, lambda peer: sum_send.at[buffers, peer], sum_recv.at[buffers])
        sum_recv[buffers, me] = sum_send[buffers, me]
        arrive(phase, sum_recv.at[buffers])
        return jnp.sum(sum_recv[buffers].astype(F32), axis=0)

    def share_rows(phase, buffers, mine, gain):
        row_send[buffers] = mine
        start(phase, lambda peer: row_send.at[buffers], row_recv.at[buffers])
        row_recv[buffers, me] = mine
        arrive(phase, row_recv.at[buffers])
        for d in range(n):
            wide[:, d * feat : (d + 1) * feat] = row_recv[buffers, d].astype(F32)
        whole = wide[...]
        spread = jnp.mean(whole * whole, axis=-1, keepdims=True)
        act_in[...] = (whole * lax.rsqrt(spread + 1e-06) * gain[...]).astype(BF16)

    loads[2].wait()

    def project(c):
        cols = pl.ds(pl.multiple_of(c * n_step, n_step), n_step)
        flat[:, cols] = jnp.dot(context, out_w[:, cols], preferred_element_type=F32)

    each(0, width // n_step, project)
    carried = (residual[...].astype(F32) + reduce_over(SUM_A, 0)).astype(BF16)
    share_rows(ROW_A, 0, carried, ffn_gain)

    hidden = gate_w.shape[0]

    def expand(c, sums):
        gate_load(c).wait()
        up_load(c).wait()
        at = pl.ds(pl.multiple_of(c * k_step, k_step), k_step)
        piece = act_in[:, at]
        return (
            sums[0] + dot_rows(piece, gate_w[:, at]),
            sums[1] + dot_rows(piece, up_w[:, at]),
        )

    zero = jnp.zeros((seqs, hidden), F32)
    gate, up = lax.fori_loop(0, width // k_step, expand, (zero, zero))
    activated = (gate / (1.0 + jnp.exp(-gate)) * up).astype(BF16)

    def contract(c):
        down_load(c).wait()
        cols = pl.ds(pl.multiple_of(c * n_step, n_step), n_step)
        flat[:, cols] = jnp.dot(activated, down_w[:, cols], preferred_element_type=F32)

    each(0, width // n_step, contract)
    leaving = (carried.astype(F32) + reduce_over(SUM_B, 1)).astype(BF16)
    hidden_out[...] = leaving
    share_rows(ROW_B, 1, leaving, query_gain)

    loads[3].wait()

    def ask(c, total):
        at = pl.ds(pl.multiple_of(c * k_step, k_step), k_step)
        return total + dot_rows(act_in[:, at], query_w[:, at])

    fresh = lax.fori_loop(0, width // k_step, ask, jnp.zeros((seqs, feat), F32))
    fresh = (fresh + query_bias[...]).astype(BF16).astype(F32)

    def address(d):
        row = jnp.zeros((1, feat), F32)
        for s in range(seqs):
            row = row + jnp.where(home[s] == d, fresh[s : s + 1], 0.0)
        home_send[d] = row.astype(BF16)

    for d in range(n):
        address(d)
    start(HOME, lambda peer: home_send.at[peer], home_recv)
    home_recv[me] = home_send[me]
    arrive(HOME, home_recv)
    for d in range(n):
        wide[0:1, d * feat : (d + 1) * feat] = home_recv[d].astype(F32)
    next_out[...] = wide[0:1, :].astype(BF16)

    finish(send_sem, ASK, asked)
    finish(send_sem, MERGE, merge_recv)
    finish(send_sem, SUM_A, sum_recv.at[0])
    finish(send_sem, ROW_A, row_recv.at[0])
    finish(send_sem, SUM_B, sum_recv.at[1])
    finish(send_sem, ROW_B, row_recv.at[1])
    finish(send_sem, HOME, home_recv)


def local(
    n,
    queries,
    home_device,
    lengths,
    key_cache,
    value_cache,
    residual,
    out_weight,
    ffn_gain,
    gate_weight,
    up_weight,
    down_weight,
    query_gain,
    query_weight,
    query_bias,
):
    seqs, feat = residual.shape
    width = queries.shape[1]
    packed = pl.cdiv(feat, 128) * 128 + 128
    step = chunks_of(width, 128, 512)
    vmem = pl.BlockSpec(memory_space=pltpu.VMEM)
    smem = pl.BlockSpec(memory_space=pltpu.SMEM)
    left = pl.BlockSpec(memory_space=pl.ANY)
    dma = pltpu.SemaphoreType.DMA

    def like(array):
        return pltpu.VMEM(array.shape, array.dtype)

    def flipped(array):
        return pltpu.VMEM(array.shape[::-1], array.dtype)

    return pl.pallas_call(
        functools.partial(kernel, n),
        out_shape=(
            jax.ShapeDtypeStruct((seqs, feat), BF16),
            jax.ShapeDtypeStruct((1, width), BF16),
        ),
        in_specs=[smem] * 2 + [vmem] * 5 + [left] * 7,
        out_specs=(vmem, vmem),
        scratch_shapes=[
            like(key_cache),
            like(value_cache),
            like(out_weight),
            flipped(gate_weight),
            flipped(up_weight),
            like(down_weight),
            flipped(query_weight),
            pltpu.VMEM((n, 1, width), BF16),
            pltpu.VMEM((seqs, KVH, 8, HEAD), F32),
            pltpu.VMEM((seqs, width), F32),
            pltpu.VMEM((seqs, 128), F32),
            pltpu.VMEM((n, seqs, packed), F32),
            pltpu.VMEM((n, seqs, packed), F32),
            pltpu.VMEM((2, n, seqs, feat), BF16),
            pltpu.VMEM((2, n, seqs, feat), BF16),
            pltpu.VMEM((2, seqs, feat), BF16),
            pltpu.VMEM((2, n, seqs, feat), BF16),
            pltpu.VMEM((n, 1, feat), BF16),
            pltpu.VMEM((n, 1, feat), BF16),
            pltpu.VMEM((seqs, width), F32),
            pltpu.VMEM((seqs, width), BF16),
            dma((4,)),
            dma((width // step,)),
            dma((width // step,)),
            dma((width // step,)),
            dma((7,)),
            dma((7,)),
        ],
        compiler_params=pltpu.CompilerParams(
            collective_id=0, has_side_effects=True, vmem_limit_bytes=67043328
        ),
        name="decode_step",
    )(
        home_device,
        lengths,
        queries,
        residual,
        ffn_gain[None, :],
        query_gain[None, :],
        query_bias[None, :],
        key_cache,
        value_cache,
        out_weight,
        gate_weight.T,
        up_weight.T,
        down_weight,
        query_weight.T,
    )


def solution(mesh):
    placed = (
        P(("grp", "blk"), None),
        P("grp"),
        P("grp"),
        P("grp", "blk", None),
        P("grp", "blk", None),
        P("grp", "blk"),
        P("blk", None),
        P(),
        P(None, "blk"),
        P(None, "blk"),
        P("blk", None),
        P(),
        P(None, "blk"),
        P("blk"),
    )
    return jax.shard_map(
        functools.partial(local, mesh.shape["blk"]),
        mesh=mesh,
        in_specs=placed,
        out_specs=(P("grp", "blk"), P(("grp", "blk"), None)),
        check_vma=False,
    )
```
